512 devices in a mesh: cond: 2 (over core), kern: 8 (over y, x_hi), tile: 32 (over x_lo, z).
Axes of the slice: x: 4 (x_hi: 2, x_lo: 2; x = x_hi * 2 + x_lo), y: 4, z: 16, core: 2. Of those that a mesh axis runs over, the one named last changes fastest.
Arguments:
- mask: bfloat16 [1, 1024, 1024], P(None, 'tile'), may hold values from -6 to 6
- kernels: bfloat16 [2, 4, 24, 512, 512], P(None, 'cond', 'kern', 'tile'), may hold values from -6 to 6
- kernel_weights: float32 [4, 24], P('cond', 'kern'), may hold values from 0.02 to 0.2
Outputs:
- low: float32 [1, 1024, 1024], P(None, 'tile', 'kern')
- high: float32 [1, 1024, 1024], P(None, 'tile', 'kern')
The draws below stay inside these ranges and needn't reach their ends.
All inputs are finite; a program needn't handle non-finite values.
Results may differ from the reference program's by a relative error of at most 0.0032.
Values may be sent and summed in bfloat16 or wider, within the bound.
No kernel may reach another device: no remote copies, remote signals or barrier semaphores. Data moves between devices by JAX's collectives and lax.ppermute only.
A program may use at most 64 MiB of HBM per device.

```python
import math
import jax
import jax.numpy as jnp
from jax import lax

P_SIZE = 1024
B = 512
KERNELS = 24
CONDS = 4
TILES = 1


def steps_of(own_key, shape, split, smallest, largest):
    factor_of = 1.0
    for dim, parts in split:
        steps = jax.random.uniform(jax.random.fold_in(jax.random.fold_in(own_key, 6), dim), (parts,), jnp.float32, smallest / len(split), largest / len(split))
        factor_of = factor_of * jnp.repeat(jnp.exp(steps), shape[dim] // parts).reshape((-1,) + (1,) * (len(shape) - 1 - dim))
    return factor_of


def normal_values(own_key, dims, scale, most, split=(), held_as=jnp.bfloat16):
    values = scale * jax.random.normal(own_key, dims, jnp.float32)
    if split:
        values = values * steps_of(own_key, dims, split, -0.22, 0.18)
    return jnp.clip(values, -most, most).astype(held_as)


def setup_inputs(seed: int = 0) -> dict:
    keys = jax.random.split(jax.random.key(seed), 4)
    return {
        "mask": normal_values(keys[0], (TILES, P_SIZE, P_SIZE), 1.0, 6.0, ((1, 32),)),
        "kernels": normal_values(keys[1], (2, CONDS, KERNELS, B, B), 1.0, 6.0, ((1, 2), (2, 8), (3, 32))),
        "kernel_weights": jnp.clip(jnp.exp(math.log(0.2) - 2.3025851 * jax.random.uniform(keys[2], (CONDS, KERNELS), jnp.float32) ** steps_of(keys[2], (CONDS, KERNELS), ((0, 2), (1, 8)), -0.2, 0.2)), 0.02, 0.2),
    }


def tables(length, count):
    pixel = jnp.arange(length, dtype=jnp.int32)[:, None]
    freq = jnp.arange(count, dtype=jnp.int32)[None, :] - count // 2
    phase = jnp.mod(pixel * freq, length).astype(jnp.float32) * (2.0 * math.pi / length)
    factor = 1.0 / math.sqrt(length)
    return ((jnp.cos(phase) * factor).astype(jnp.bfloat16), (jnp.sin(phase) * factor).astype(jnp.bfloat16))

def product(left, right):
    return jnp.dot(left, right, preferred_element_type=jnp.float32)

def reference(mask, kernels, kernel_weights):
    cos_table, sin_table = tables(P_SIZE, B)
    cos_back = cos_table.T
    sin_back = sin_table.T

    def one_tile(tile):
        row_re = product(tile, cos_table).astype(jnp.bfloat16)
        row_im = (-product(tile, sin_table)).astype(jnp.bfloat16)
        spec_re = product(row_re.T, cos_table) + product(row_im.T, sin_table)
        spec_im = product(row_im.T, cos_table) - product(row_re.T, sin_table)

        def one_cond(inputs):
            cond_re, cond_im, weights = inputs

            def add_kernel(total, item):
                kern_re, kern_im, weight = item
                kern_re = kern_re.astype(jnp.float32)
                kern_im = kern_im.astype(jnp.float32)
                filt_re = (spec_re * kern_re - spec_im * kern_im).astype(jnp.bfloat16)
                filt_im = (spec_re * kern_im + spec_im * kern_re).astype(jnp.bfloat16)
                half_re = (product(filt_re, cos_back) - product(filt_im, sin_back)).astype(jnp.bfloat16)
                half_im = (product(filt_re, sin_back) + product(filt_im, cos_back)).astype(jnp.bfloat16)
                field_re = product(half_re.T, cos_back) - product(half_im.T, sin_back)
                field_im = product(half_re.T, sin_back) + product(half_im.T, cos_back)
                return (total + weight * (field_re * field_re + field_im * field_im), None)
            start = jnp.zeros((P_SIZE, P_SIZE), jnp.float32)
            total, _ = lax.scan(add_kernel, start, (cond_re, cond_im, weights))
            return total
        intensity = lax.map(one_cond, (kernels[0], kernels[1], kernel_weights))
        return (lax.optimization_barrier(jnp.min(intensity, axis=0)), lax.optimization_barrier(jnp.max(intensity, axis=0)))
    low, high = lax.map(one_tile, mask)
    return (low, high)
```

```python
import math

import jax
import jax.numpy as jnp
import numpy as np
from jax import lax
from jax.experimental import pallas as pl
from jax.experimental.pallas import tpu as pltpu
from jax.sharding import PartitionSpec as P

BF = jnp.bfloat16
F32 = jnp.float32
TN = (((0,), (0,)), ((), ()))
NN = (((1,), (0,)), ((), ()))
NT = (((1,), (1,)), ((), ()))


def tables(length, count):
    pixel = np.arange(length, dtype=np.int64)[:, None]
    freq = np.arange(count, dtype=np.int64)[None, :] - count // 2
    phase = np.mod(pixel * freq, length).astype(np.float32) * np.float32(2.0 * math.pi / length)
    factor = np.float32(1.0 / math.sqrt(length))
    return (
        (np.cos(phase) * factor).astype(BF),
        (np.sin(phase) * factor).astype(BF),
    )


def dot(a, b, dims):
    return lax.dot_general(a, b, dims, preferred_element_type=F32)


def regroup(blocks, lanes):
    group = (lax.broadcasted_iota(jnp.int32, blocks[0].shape, 1) // 32) % 4
    outs = []
    for b in range(4):
        moved = [
            blk if q == b else pltpu.roll(blk, (32 * (q - b)) % lanes, 1)
            for q, blk in enumerate(blocks)
        ]
        low = jnp.where(group == 0, moved[0], moved[1])
        high = jnp.where(group == 2, moved[2], moved[3])
        outs.append(jnp.where(group < 2, low, high))
    return outs


def rows_kernel(mask_ref, table_ref, sign_ref, out_ref):
    rows, pixels = mask_ref.shape
    half = pixels // 2
    both = jnp.concatenate([mask_ref[:, :half], mask_ref[:, half:]], axis=0)
    part = dot(both, table_ref[...], NN)
    out = part[:rows] + part[rows:] * sign_ref[...]
    width = out.shape[1] // 4
    stacked = jnp.concatenate([out[:, g * width : (g + 1) * width] for g in range(4)], axis=0)
    out_ref[...] = stacked.T.astype(BF)


def half_kernel(cols_ref, kern_ref, table_ref, out_ref):
    tiles = cols_ref.shape[0] // 8
    count = kern_ref.shape[3]
    cols = cols_ref[...].astype(F32).reshape(tiles // 4, 4, 8, 128)
    blocks = [
        jnp.concatenate([cols[D, b] for D in range(tiles // 4)], axis=1) for b in range(4)
    ]
    groups = regroup(blocks, 32 * tiles)
    lines = jnp.concatenate(groups, axis=0).astype(BF)
    part = dot(lines, table_ref[...], NN)
    spec_re = part[:16, :count] + part[16:, count:]
    spec_im = part[16:, :count] - part[:16, count:]
    top, low = [], []
    items = kern_ref.shape[1]
    for n in range(items):
        kre = kern_ref[0, n].astype(F32)
        kim = kern_ref[1, n].astype(F32)
        fre = (spec_re * kre - spec_im * kim).astype(BF)
        fim = (spec_re * kim + spec_im * kre).astype(BF)
        top.append(jnp.concatenate([fre, -fim], axis=1))
        low.append(jnp.concatenate([fim, fre], axis=1))
    lhs = jnp.concatenate(top + low, axis=0)
    fields = dot(lhs, table_ref[...], NT)
    pick = lambda ri, n: fields[(ri * items + n) * 16 : (ri * items + n + 1) * 16]
    quads = (
        [pick(0, n) for n in range(4)],
        [pick(1, n) for n in range(4)],
        [pick(0, 4), pick(0, 5), pick(1, 4), pick(1, 5)],
    )
    for at, quad in enumerate(quads):
        for b, moved in enumerate(regroup(quad, 32 * tiles)):
            moved = moved.astype(BF)
            for D in range(tiles // 4):
                out_ref[4 * D + b, 16 * at : 16 * at + 16] = moved[:, 128 * D : 128 * D + 128]


def power_kernel(half_ref, weight_ref, table_ref, out_ref):
    tiles = half_ref.shape[0]
    conds, kerns = weight_ref.shape
    quad = [half_ref[:, 16 * q : 16 * q + 16, :].reshape(16 * tiles, 128).T for q in range(3)]
    half_re = jnp.concatenate([quad[0], quad[2][:64]], axis=0)
    half_im = jnp.concatenate([quad[1], quad[2][64:]], axis=0)
    field_re = dot(jnp.concatenate([half_re, -half_im], axis=1), table_ref[...], NT)
    field_im = dot(jnp.concatenate([half_im, half_re], axis=1), table_ref[...], NT)
    power = field_re * field_re + field_im * field_im
    for c in range(conds):
        total = None
        for k in range(kerns):
            n = c * kerns + k
            term = power[32 * n : 32 * n + 32] * weight_ref[c, k]
            total = term if total is None else total + term
        for d in range(out_ref.shape[0]):
            out_ref[d, 32 * c : 32 * c + 32] = total[:, 128 * d : 128 * d + 128]


def bounds_kernel(parts_ref, out_ref):
    total = parts_ref[0]
    for s in range(1, parts_ref.shape[0]):
        total = total + parts_ref[s]
    out_ref[:32] = jnp.minimum(total[:32], total[32:])
    out_ref[32:] = jnp.maximum(total[:32], total[32:])


def call(body, shape, dtype, *args, smem=()):
    return pl.pallas_call(
        body,
        out_shape=jax.ShapeDtypeStruct(shape, dtype),
        in_specs=[
            pl.BlockSpec(memory_space=pltpu.SMEM if n in smem else pltpu.VMEM)
            for n in range(len(args))
        ],
        out_specs=pl.BlockSpec(memory_space=pltpu.VMEM),
        compiler_params=pltpu.CompilerParams(vmem_limit_bytes=48 * 1024 * 1024),
        name=body.__name__,
    )(*args)


def local(mask, kernels, kernel_weights):
    _, rows, pixels = mask.shape
    conds, kerns = kernel_weights.shape
    count = kernels.shape[4]
    tiles, groups = lax.axis_size("tile"), lax.axis_size("kern")
    cos_table, sin_table = tables(pixels, count)
    table = jnp.asarray(np.concatenate([cos_table, sin_table], axis=1))
    order = np.arange(count).reshape(tiles, 2, 8).transpose(1, 0, 2).reshape(-1)
    row_table = np.concatenate([cos_table[:, order], -sin_table[:, order]], axis=1)
    sign = np.where((order - count // 2) % 2 == 0, 1.0, -1.0).astype(np.float32)
    row_table = jnp.asarray(row_table[: pixels // 2])
    sign = jnp.asarray(np.concatenate([sign, sign])[None])

    sent = call(rows_kernel, (8 * tiles, 128), BF, mask[0], row_table, sign)
    cols = lax.all_to_all(sent, "tile", split_axis=0, concat_axis=0, tiled=True)
    kern = kernels.reshape(2, conds * kerns, kernels.shape[3], count)
    half = call(half_kernel, (tiles, 48, 128), BF, cols, kern, table)
    half = lax.all_to_all(half, "tile", split_axis=0, concat_axis=0, tiled=True)
    weighted = call(power_kernel, (groups, 64, 128), F32, half, kernel_weights, table, smem=(1,))
    parts = lax.all_to_all(weighted, "kern", split_axis=0, concat_axis=0, tiled=True)
    band = call(bounds_kernel, (64, 128), F32, parts)
    bands = lax.all_gather(band, "cond")
    low = jnp.minimum(bands[0, :32], bands[1, :32])
    high = jnp.maximum(bands[0, 32:], bands[1, 32:])
    return (low[None], high[None])


def solution(mesh):
    placed = (P(None, "tile", None), P(None, "cond", "kern", "tile", None), P("cond", "kern"))
    return jax.shard_map(
        local,
        mesh=mesh,
        in_specs=placed,
        out_specs=(P(None, "tile", "kern"), P(None, "tile", "kern")),
        check_vma=False,
    )
```

```python
import math

import jax
import jax.numpy as jnp
import numpy as np
from jax import lax
from jax.experimental import pallas as pl
from jax.experimental.pallas import tpu as pltpu
from jax.sharding import PartitionSpec as P

BF = jnp.bfloat16
F32 = jnp.float32
TN = (((0,), (0,)), ((), ()))
NN = (((1,), (0,)), ((), ()))
NT = (((1,), (1,)), ((), ()))


def tables(length, count):
    pixel = np.arange(length, dtype=np.int64)[:, None]
    freq = np.arange(count, dtype=np.int64)[None, :] - count // 2
    phase = np.mod(pixel * freq, length).astype(np.float32) * np.float32(2.0 * math.pi / length)
    factor = np.float32(1.0 / math.sqrt(length))
    return (
        (np.cos(phase) * factor).astype(BF),
        (np.sin(phase) * factor).astype(BF),
    )


def dot(a, b, dims):
    return lax.dot_general(a, b, dims, preferred_element_type=F32)


def regroup(blocks, lanes):
    group = (lax.broadcasted_iota(jnp.int32, blocks[0].shape, 1) // 32) % 4
    outs = []
    for b in range(4):
        moved = [
            blk if q == b else pltpu.roll(blk, (32 * (q - b)) % lanes, 1)
            for q, blk in enumerate(blocks)
        ]
        low = jnp.where(group == 0, moved[0], moved[1])
        high = jnp.where(group == 2, moved[2], moved[3])
        outs.append(jnp.where(group < 2, low, high))
    return outs


def rows_kernel(
    mask_ref, rows_ref, table_ref, kern_ref, out_ref, table_out, kern_out, mask_buf, table_buf, sems
):
    pairs = [(mask_ref, mask_buf), (rows_ref, table_buf), (table_ref, table_out), (kern_ref, kern_out)]
    copies = [pltpu.make_async_copy(src, dst, sems.at[n]) for n, (src, dst) in enumerate(pairs)]
    for copy in copies:
        copy.start()
    for copy in copies[:2]:
        copy.wait()
    rows, pixels = mask_buf.shape
    half = pixels // 2
    both = jnp.concatenate([mask_buf[:, :half], mask_buf[:, half:]], axis=0)
    part = dot(both, table_buf[...], NN)
    odd = lax.broadcasted_iota(jnp.int32, (rows, part.shape[1]), 1) % 2 == 1
    out = part[:rows] + jnp.where(odd, -part[rows:], part[rows:])
    width = out.shape[1] // 4
    stacked = jnp.concatenate([out[:, g * width : (g + 1) * width] for g in range(4)], axis=0)
    out_ref[...] = stacked.T.astype(BF)
    for copy in copies[2:]:
        copy.wait()


def half_kernel(cols_ref, kern_ref, table_ref, out_ref):
    tiles = cols_ref.shape[0] // 8
    count = kern_ref.shape[3]
    cols = cols_ref[...].astype(F32).reshape(tiles // 4, 4, 8, 128)
    blocks = [
        jnp.concatenate([cols[D, b] for D in range(tiles // 4)], axis=1) for b in range(4)
    ]
    groups = regroup(blocks, 32 * tiles)
    lines = jnp.concatenate(groups, axis=0).astype(BF)
    part = dot(lines, table_ref[...], NN)
    spec_re = part[:16, :count] + part[16:, count:]
    spec_im = part[16:, :count] - part[:16, count:]
    top, low = [], []
    items = kern_ref.shape[1]
    for n in range(items):
        kre = kern_ref[0, n].astype(F32)
        kim = kern_ref[1, n].astype(F32)
        fre = (spec_re * kre - spec_im * kim).astype(BF)
        fim = (spec_re * kim + spec_im * kre).astype(BF)
        top.append(jnp.concatenate([fre, -fim], axis=1))
        low.append(jnp.concatenate([fim, fre], axis=1))
    lhs = jnp.concatenate(top + low, axis=0)
    fields = dot(lhs, table_ref[...], NT)
    pick = lambda ri, n: fields[(ri * items + n) * 16 : (ri * items + n + 1) * 16]
    quads = (
        [pick(0, n) for n in range(4)],
        [pick(1, n) for n in range(4)],
        [pick(0, 4), pick(0, 5), pick(1, 4), pick(1, 5)],
    )
    for at, quad in enumerate(quads):
        for b, moved in enumerate(regroup(quad, 32 * tiles)):
            moved = moved.astype(BF)
            for D in range(tiles // 4):
                out_ref[4 * D + b, 16 * at : 16 * at + 16] = moved[:, 128 * D : 128 * D + 128]


def power_kernel(half_ref, weight_ref, table_ref, out_ref):
    tiles = half_ref.shape[0]
    conds, kerns = weight_ref.shape
    quad = [half_ref[:, 16 * q : 16 * q + 16, :].reshape(16 * tiles, 128).T for q in range(3)]
    half_re = jnp.concatenate([quad[0], quad[2][:64]], axis=0)
    half_im = jnp.concatenate([quad[1], quad[2][64:]], axis=0)
    field_re = dot(jnp.concatenate([half_re, -half_im], axis=1), table_ref[...], NT)
    field_im = dot(jnp.concatenate([half_im, half_re], axis=1), table_ref[...], NT)
    power = field_re * field_re + field_im * field_im
    for c in range(conds):
        total = None
        for k in range(kerns):
            n = c * kerns + k
            term = power[32 * n : 32 * n + 32] * weight_ref[c, k]
            total = term if total is None else total + term
        total = total.astype(BF)
        for d in range(out_ref.shape[0]):
            at = d % (total.shape[1] // 128) * 128
            out_ref[d, 32 * c : 32 * c + 32] = total[:, at : at + 128]


def bounds_kernel(parts_ref, low_ref, high_ref):
    halves = []
    kern = parts_ref.shape[0] // 2
    for group in range(2):
        total = parts_ref[group * kern].astype(F32)
        for s in range(1, kern):
            total = total + parts_ref[group * kern + s].astype(F32)
        halves += [total[:32], total[32:]]
    low_ref[...] = jnp.minimum(jnp.minimum(halves[0], halves[1]), jnp.minimum(halves[2], halves[3]))
    high_ref[...] = jnp.maximum(jnp.maximum(halves[0], halves[1]), jnp.maximum(halves[2], halves[3]))


def call(body, shapes, *args, spaces={}, scratch=(), cost=None):
    return pl.pallas_call(
        body,
        out_shape=shapes,
        in_specs=[
            pl.BlockSpec(memory_space=spaces.get(n, pltpu.VMEM)) for n in range(len(args))
        ],
        out_specs=jax.tree.map(lambda _: pl.BlockSpec(memory_space=pltpu.VMEM), shapes),
        scratch_shapes=scratch,
        cost_estimate=cost,
        compiler_params=pltpu.CompilerParams(vmem_limit_bytes=48 * 1024 * 1024),
        name=body.__name__,
    )(*args)


def local(mask, kernels, kernel_weights):
    _, rows, pixels = mask.shape
    conds, kerns = kernel_weights.shape
    count = kernels.shape[4]
    tiles, groups = lax.axis_size("tile"), lax.axis_size("kern") * lax.axis_size("cond")
    cos_table, sin_table = tables(pixels, count)
    table = jnp.asarray(np.concatenate([cos_table, sin_table], axis=1))
    order = np.arange(count).reshape(tiles, 2, 8).transpose(1, 0, 2).reshape(-1)
    row_table = np.concatenate([cos_table[:, order], -sin_table[:, order]], axis=1)
    row_table = jnp.asarray(row_table[: pixels // 2])
    shape = jax.ShapeDtypeStruct

    kern = kernels.reshape(2, conds * kerns, kernels.shape[3], count)
    sent, table, kern = call(
        rows_kernel,
        (shape((8 * tiles, 128), BF), shape(table.shape, BF), shape(kern.shape, BF)),
        *(pltpu.with_memory_space_constraint(a, pltpu.HBM) for a in (mask[0], row_table, table, kern)),
        spaces={n: pltpu.HBM for n in range(4)},
        scratch=[
            pltpu.VMEM((rows, pixels), BF),
            pltpu.VMEM(row_table.shape, BF),
            pltpu.SemaphoreType.DMA((4,)),
        ],
    )
    cols = lax.all_to_all(sent, "tile", split_axis=0, concat_axis=0, tiled=True)
    half = call(half_kernel, shape((tiles, 48, 128), BF), cols, kern, table)
    half = lax.all_to_all(half, "tile", split_axis=0, concat_axis=0, tiled=True)
    weighted = call(
        power_kernel, shape((groups, 64, 128), BF), half, kernel_weights, table, spaces={1: pltpu.SMEM}
    )
    parts = lax.all_to_all(weighted, ("cond", "kern"), split_axis=0, concat_axis=0, tiled=True)
    low, high = call(bounds_kernel, (shape((32, 128), F32),) * 2, parts)
    return (low[None], high[None])


def solution(mesh):
    placed = (P(None, "tile", None), P(None, "cond", "kern", "tile", None), P("cond", "kern"))
    return jax.shard_map(
        local,
        mesh=mesh,
        in_specs=placed,
        out_specs=(P(None, "tile", "kern"), P(None, "tile", "kern")),
        check_vma=False,
    )
```

```python
import functools
import math

import jax
import jax.numpy as jnp
import numpy as np
from jax import lax
from jax.experimental import pallas as pl
from jax.experimental.pallas import tpu as pltpu
from jax.sharding import PartitionSpec as P

BF = jnp.bfloat16
F32 = jnp.float32
TN = (((0,), (0,)), ((), ()))
NN = (((1,), (0,)), ((), ()))
NT = (((1,), (1,)), ((), ()))


def rotated(count, first):
    return [(first + at) % count for at in range(count)]


def tables(length, count):
    pixel = np.arange(length, dtype=np.int64)[:, None]
    freq = np.arange(count, dtype=np.int64)[None, :] - count // 2
    phase = np.mod(pixel * freq, length).astype(np.float32) * np.float32(2.0 * math.pi / length)
    factor = np.float32(1.0 / math.sqrt(length))
    return (
        (np.cos(phase) * factor).astype(BF),
        (np.sin(phase) * factor).astype(BF),
    )


def dot(a, b, dims):
    return lax.dot_general(a, b, dims, preferred_element_type=F32)


def regroup(blocks, lanes):
    group = (lax.broadcasted_iota(jnp.int32, blocks[0].shape, 1) // 32) % 4
    outs = []
    for b in range(4):
        moved = [
            blk if q == b else pltpu.roll(blk, (32 * (q - b)) % lanes, 1)
            for q, blk in enumerate(blocks)
        ]
        low = jnp.where(group == 0, moved[0], moved[1])
        high = jnp.where(group == 2, moved[2], moved[3])
        outs.append(jnp.where(group < 2, low, high))
    return outs


def rows_kernel(
    mask_ref, rows_ref, table_ref, kern_ref, out_ref, table_out, kern_out, mask_buf, table_buf, sems
):
    pairs = [(mask_ref, mask_buf), (rows_ref, table_buf), (table_ref, table_out), (kern_ref, kern_out)]
    copies = [pltpu.make_async_copy(src, dst, sems.at[n]) for n, (src, dst) in enumerate(pairs)]
    for copy in copies:
        copy.start()
    for copy in copies[:2]:
        copy.wait()
    rows, pixels = mask_buf.shape
    half = pixels // 2
    both = jnp.concatenate([mask_buf[:, :half], mask_buf[:, half:]], axis=0)
    part = dot(both, table_buf[...], NN)
    odd = lax.broadcasted_iota(jnp.int32, (rows, part.shape[1]), 1) % 2 == 1
    out = part[:rows] + jnp.where(odd, -part[rows:], part[rows:])
    width = out.shape[1] // 4
    stacked = jnp.concatenate([out[:, g * width : (g + 1) * width] for g in range(4)], axis=0)
    out_ref[...] = stacked.T.astype(BF)
    for copy in copies[2:]:
        copy.wait()


def half_kernel(cols_ref, kern_ref, table_ref, out_ref, *, came, goes):
    tiles = cols_ref.shape[0] // 8
    count = kern_ref.shape[3]
    cols = cols_ref[...].astype(F32).reshape(tiles, 8, 128)
    blocks = [
        jnp.concatenate([cols[came[4 * D + b]] for D in range(tiles // 4)], axis=1) for b in range(4)
    ]
    groups = regroup(blocks, 32 * tiles)
    lines = jnp.concatenate(groups, axis=0).astype(BF)
    part = dot(lines, table_ref[...], NT)
    spec_re = part[:16, :count] + part[16:, count:]
    spec_im = part[16:, :count] - part[:16, count:]
    top, low = [], []
    items = kern_ref.shape[1]
    for n in range(items):
        kre = kern_ref[0, n].astype(F32)
        kim = kern_ref[1, n].astype(F32)
        fre = (spec_re * kre - spec_im * kim).astype(BF)
        fim = (spec_re * kim + spec_im * kre).astype(BF)
        top.append(jnp.concatenate([fre, -fim], axis=1))
        low.append(jnp.concatenate([fim, fre], axis=1))
    lhs = jnp.concatenate(top + low, axis=0)
    fields = dot(lhs, table_ref[...], NN)
    pick = lambda ri, n: fields[(ri * items + n) * 16 : (ri * items + n + 1) * 16]
    quads = (
        [pick(0, n) for n in range(4)],
        [pick(1, n) for n in range(4)],
        [pick(0, 4), pick(0, 5), pick(1, 4), pick(1, 5)],
    )
    for at, quad in enumerate(quads):
        for b, moved in enumerate(regroup(quad, 32 * tiles)):
            moved = moved.astype(BF)
            for D in range(tiles // 4):
                out_ref[goes[4 * D + b], 16 * at : 16 * at + 16] = moved[:, 128 * D : 128 * D + 128]


def power_kernel(half_ref, weight_ref, table_ref, out_ref, *, came, goes):
    tiles = half_ref.shape[0]
    conds, kerns = weight_ref.shape
    half = [half_ref[came[t]] for t in range(tiles)]
    quad = [jnp.concatenate([h[16 * q : 16 * q + 16] for h in half], axis=0).T for q in range(3)]
    half_re = jnp.concatenate([quad[0], quad[2][:64]], axis=0)
    half_im = jnp.concatenate([quad[1], quad[2][64:]], axis=0)
    field_re = dot(jnp.concatenate([half_re, -half_im], axis=1), table_ref[...], NN)
    field_im = dot(jnp.concatenate([half_im, half_re], axis=1), table_ref[...], NN)
    power = field_re * field_re + field_im * field_im
    for c in range(conds):
        total = None
        for k in range(kerns):
            n = c * kerns + k
            term = power[32 * n : 32 * n + 32] * weight_ref[c, k]
            total = term if total is None else total + term
        total = total.astype(BF)
        for d in range(out_ref.shape[0]):
            at = d % (total.shape[1] // 128) * 128
            out_ref[goes[d], 32 * c : 32 * c + 32] = total[:, at : at + 128]


def bounds_kernel(parts_ref, low_ref, high_ref, *, came):
    halves = []
    kern = parts_ref.shape[0] // 2
    for group in range(2):
        total = parts_ref[came[group * kern]].astype(F32)
        for s in range(1, kern):
            total = total + parts_ref[came[group * kern + s]].astype(F32)
        halves += [total[:32], total[32:]]
    low_ref[...] = jnp.minimum(jnp.minimum(halves[0], halves[1]), jnp.minimum(halves[2], halves[3]))
    high_ref[...] = jnp.maximum(jnp.maximum(halves[0], halves[1]), jnp.maximum(halves[2], halves[3]))


def call(body, shapes, *args, spaces={}, scratch=(), **places):
    return pl.pallas_call(
        functools.partial(body, **places),
        out_shape=shapes,
        in_specs=[
            pl.BlockSpec(memory_space=spaces.get(n, pltpu.VMEM)) for n in range(len(args))
        ],
        out_specs=jax.tree.map(lambda _: pl.BlockSpec(memory_space=pltpu.VMEM), shapes),
        scratch_shapes=scratch,
        compiler_params=pltpu.CompilerParams(vmem_limit_bytes=48 * 1024 * 1024),
        name=body.__name__,
    )(*args)


def swapped(blocks, axis, order):
    return lax.all_to_all(
        blocks, axis, split_axis=0, concat_axis=0, tiled=True, axis_index_groups=[order]
    )


def place(order):
    return [order.index(member) for member in range(len(order))]


def local(mask, kernels, kernel_weights):
    _, rows, pixels = mask.shape
    conds, kerns = kernel_weights.shape
    count = kernels.shape[4]
    tiles, groups = lax.axis_size("tile"), lax.axis_size("kern") * lax.axis_size("cond")
    cos_table, sin_table = tables(pixels, count)
    table = jnp.asarray(np.concatenate([cos_table, sin_table], axis=1).T)
    tile_order, image_order = rotated(tiles, 3 * tiles // 4), rotated(groups, 3 * groups // 4)
    order = np.arange(count).reshape(tiles, 2, 8)[tile_order].transpose(1, 0, 2).reshape(-1)
    row_table = np.concatenate([cos_table[:, order], -sin_table[:, order]], axis=1)
    row_table = jnp.asarray(row_table[: pixels // 2])
    shape = jax.ShapeDtypeStruct

    kern = kernels.reshape(2, conds * kerns, kernels.shape[3], count)
    sent, table, kern = call(
        rows_kernel,
        (shape((8 * tiles, 128), BF), shape(table.shape, BF), shape(kern.shape, BF)),
        *(pltpu.with_memory_space_constraint(a, pltpu.HBM) for a in (mask[0], row_table, table, kern)),
        spaces={n: pltpu.HBM for n in range(4)},
        scratch=[
            pltpu.VMEM((rows, pixels), BF),
            pltpu.VMEM(row_table.shape, BF),
            pltpu.SemaphoreType.DMA((4,)),
        ],
    )
    cols = swapped(sent, "tile", tile_order)
    half = call(
        half_kernel,
        shape((tiles, 48, 128), BF),
        cols,
        kern,
        table,
        came=place(tile_order),
        goes=place(tile_order),
    )
    half = swapped(half, "tile", tile_order)
    weighted = call(
        power_kernel,
        shape((groups, 64, 128), BF),
        half,
        kernel_weights,
        table,
        spaces={1: pltpu.SMEM},
        came=place(tile_order),
        goes=place(image_order),
    )
    parts = swapped(weighted, ("cond", "kern"), image_order)
    low, high = call(bounds_kernel, (shape((32, 128), F32),) * 2, parts, came=place(image_order))
    return (low[None], high[None])


def solution(mesh):
    placed = (P(None, "tile", None), P(None, "cond", "kern", "tile", None), P("cond", "kern"))
    return jax.shard_map(
        local,
        mesh=mesh,
        in_specs=placed,
        out_specs=(P(None, "tile", "kern"), P(None, "tile", "kern")),
        check_vma=False,
    )
```

```python
import functools
import math

import jax
import jax.numpy as jnp
import numpy as np
from jax import lax
from jax.experimental import pallas as pl
from jax.experimental.pallas import tpu as pltpu
from jax.sharding import PartitionSpec as P

BF = jnp.bfloat16
F32 = jnp.float32
TN = (((0,), (0,)), ((), ()))
NN = (((1,), (0,)), ((), ()))
NT = (((1,), (1,)), ((), ()))


def ring_order(rings, length, first, step):
    return [
        ring * length + (first + step * at) % length
        for at in range(length)
        for ring in reversed(range(rings))
    ]


def tables(length, count):
    pixel = np.arange(length, dtype=np.int64)[:, None]
    freq = np.arange(count, dtype=np.int64)[None, :] - count // 2
    phase = np.mod(pixel * freq, length).astype(np.float32) * np.float32(2.0 * math.pi / length)
    factor = np.float32(1.0 / math.sqrt(length))
    return (
        (np.cos(phase) * factor).astype(BF),
        (np.sin(phase) * factor).astype(BF),
    )


def alternated(a):
    odd = lax.broadcasted_iota(jnp.int32, a.shape, 1) % 2 == 1
    return jnp.where(odd, -a, a)


def dot(a, b, dims):
    return lax.dot_general(a, b, dims, preferred_element_type=F32)


def regroup(blocks, lanes):
    group = (lax.broadcasted_iota(jnp.int32, blocks[0].shape, 1) // 32) % 4
    outs = []
    for b in range(4):
        moved = [
            blk if q == b else pltpu.roll(blk, (32 * (q - b)) % lanes, 1)
            for q, blk in enumerate(blocks)
        ]
        low = jnp.where(group == 0, moved[0], moved[1])
        high = jnp.where(group == 2, moved[2], moved[3])
        outs.append(jnp.where(group < 2, low, high))
    return outs


def rows_kernel(
    mask_ref, rows_ref, table_ref, kern_ref, out_ref, table_out, kern_out, mask_buf, table_buf, sems
):
    pairs = [(mask_ref, mask_buf), (rows_ref, table_buf), (table_ref, table_out), (kern_ref, kern_out)]
    copies = [pltpu.make_async_copy(src, dst, sems.at[n]) for n, (src, dst) in enumerate(pairs)]
    for copy in copies:
        copy.start()
    for copy in copies[:2]:
        copy.wait()
    rows, pixels = mask_buf.shape
    half = pixels // 2
    both = jnp.concatenate([mask_buf[:, :half], mask_buf[:, half:]], axis=0)
    part = dot(both, table_buf[...], NN)
    out = part[:rows] + alternated(part[rows:])
    width = out.shape[1] // 4
    stacked = jnp.concatenate([out[:, g * width : (g + 1) * width] for g in range(4)], axis=0)
    out_ref[...] = stacked.T.astype(BF)
    for copy in copies[2:]:
        copy.wait()


def half_kernel(cols_ref, kern_ref, table_ref, out_ref, *, came, goes):
    tiles = cols_ref.shape[0] // 8
    count = kern_ref.shape[3]
    cols = cols_ref[...].astype(F32).reshape(tiles, 8, 128)
    blocks = [
        jnp.concatenate([cols[came[4 * D + b]] for D in range(tiles // 4)], axis=1) for b in range(4)
    ]
    groups = regroup(blocks, 32 * tiles)
    lines = jnp.concatenate(groups, axis=0).astype(BF)
    near = lines.shape[1] // 2
    part = dot(jnp.concatenate([lines[:, :near], lines[:, near:]], axis=0), table_ref[...], NT)
    part = part[:32] + alternated(part[32:])
    spec_re = part[:16, :count] + part[16:, count:]
    spec_im = part[16:, :count] - part[:16, count:]
    top, low = [], []
    items = kern_ref.shape[1]
    for n in range(items):
        kre = kern_ref[0, n].astype(F32)
        kim = kern_ref[1, n].astype(F32)
        fre = (spec_re * kre - spec_im * kim).astype(BF)
        fim = (spec_re * kim + spec_im * kre).astype(BF)
        top.append(jnp.concatenate([fre, -fim], axis=1))
        low.append(jnp.concatenate([fim, fre], axis=1))
    lhs = jnp.concatenate(top + low, axis=0)
    fields = dot(jnp.concatenate([lhs, alternated(lhs)], axis=0), table_ref[...], NN)
    for side in range(2):
        start = side * lhs.shape[0]
        block = [fields[start + 16 * n : start + 16 * n + 16] for n in range(2 * items)]
        quads = (block[:4], block[items : items + 4], block[4:items] + block[items + 4 :])
        for at, quad in enumerate(quads):
            for b, moved in enumerate(regroup(quad, near)):
                moved = moved.astype(BF)
                for D in range(near // 128):
                    d = side * tiles // 2 + 4 * D + b
                    out_ref[goes[d], 16 * at : 16 * at + 16] = moved[:, 128 * D : 128 * D + 128]


def power_kernel(half_ref, weight_ref, table_ref, out_ref, *, came, goes):
    tiles = half_ref.shape[0]
    conds, kerns = weight_ref.shape
    half = [half_ref[came[t]] for t in range(tiles)]
    quad = [jnp.concatenate([h[16 * q : 16 * q + 16] for h in half], axis=0).T for q in range(3)]
    half_re = jnp.concatenate([quad[0], quad[2][:64]], axis=0)
    half_im = jnp.concatenate([quad[1], quad[2][64:]], axis=0)
    lhs_re = jnp.concatenate([half_re, -half_im], axis=1)
    lhs_im = jnp.concatenate([half_im, half_re], axis=1)
    lhs = jnp.concatenate([lhs_re, lhs_im, alternated(lhs_re), alternated(lhs_im)], axis=0)
    fields = dot(lhs, table_ref[...], NN)
    count = half_re.shape[0]
    near = fields.shape[1] // 128
    for side in range(2):
        field_re = fields[2 * side * count : (2 * side + 1) * count]
        field_im = fields[(2 * side + 1) * count : (2 * side + 2) * count]
        power = field_re * field_re + field_im * field_im
        for c in range(conds):
            total = None
            for k in range(kerns):
                n = c * kerns + k
                term = power[32 * n : 32 * n + 32] * weight_ref[c, k]
                total = term if total is None else total + term
            total = total.astype(BF)
            for d in range(out_ref.shape[0]):
                if d % (2 * near) // near == side:
                    at = d % near * 128
                    out_ref[goes[d], 32 * c : 32 * c + 32] = total[:, at : at + 128]


def bounds_kernel(parts_ref, low_ref, high_ref, *, came):
    halves = []
    kern = parts_ref.shape[0] // 2
    for group in range(2):
        total = parts_ref[came[group * kern]].astype(F32)
        for s in range(1, kern):
            total = total + parts_ref[came[group * kern + s]].astype(F32)
        halves += [total[:32], total[32:]]
    low_ref[...] = jnp.minimum(jnp.minimum(halves[0], halves[1]), jnp.minimum(halves[2], halves[3]))
    high_ref[...] = jnp.maximum(jnp.maximum(halves[0], halves[1]), jnp.maximum(halves[2], halves[3]))


def call(body, shapes, *args, spaces={}, scratch=(), **places):
    return pl.pallas_call(
        functools.partial(body, **places),
        out_shape=shapes,
        in_specs=[
            pl.BlockSpec(memory_space=spaces.get(n, pltpu.VMEM)) for n in range(len(args))
        ],
        out_specs=jax.tree.map(lambda _: pl.BlockSpec(memory_space=pltpu.VMEM), shapes),
        scratch_shapes=scratch,
        compiler_params=pltpu.CompilerParams(vmem_limit_bytes=48 * 1024 * 1024),
        name=body.__name__,
    )(*args)


def swapped(blocks, axis, order):
    return lax.all_to_all(
        blocks, axis, split_axis=0, concat_axis=0, tiled=True, axis_index_groups=[order]
    )


def place(order):
    return [order.index(member) for member in range(len(order))]


def local(mask, kernels, kernel_weights):
    _, rows, pixels = mask.shape
    conds, kerns = kernel_weights.shape
    count = kernels.shape[4]
    tiles, groups = lax.axis_size("tile"), lax.axis_size("kern") * lax.axis_size("cond")
    cos_table, sin_table = tables(pixels, count)
    table = jnp.asarray(np.concatenate([cos_table, sin_table], axis=1)[: pixels // 2].T)
    tile_order = ring_order(2, tiles // 2, 10, 7)
    image_order = ring_order(1, groups, 13, 1)
    order = np.arange(count).reshape(tiles, 2, 8)[tile_order].transpose(1, 0, 2).reshape(-1)
    row_table = np.concatenate([cos_table[:, order], -sin_table[:, order]], axis=1)
    row_table = jnp.asarray(row_table[: pixels // 2])
    shape = jax.ShapeDtypeStruct

    kern = kernels.reshape(2, conds * kerns, kernels.shape[3], count)
    sent, table, kern = call(
        rows_kernel,
        (shape((8 * tiles, 128), BF), shape(table.shape, BF), shape(kern.shape, BF)),
        *(pltpu.with_memory_space_constraint(a, pltpu.HBM) for a in (mask[0], row_table, table, kern)),
        spaces={n: pltpu.HBM for n in range(4)},
        scratch=[
            pltpu.VMEM((rows, pixels), BF),
            pltpu.VMEM(row_table.shape, BF),
            pltpu.SemaphoreType.DMA((4,)),
        ],
    )
    cols = swapped(sent, "tile", tile_order)
    half = call(
        half_kernel,
        shape((tiles, 48, 128), BF),
        cols,
        kern,
        table,
        came=place(tile_order),
        goes=place(tile_order),
    )
    half = swapped(half, "tile", tile_order)
    weighted = call(
        power_kernel,
        shape((groups, 64, 128), BF),
        half,
        kernel_weights,
        table,
        spaces={1: pltpu.SMEM},
        came=place(tile_order),
        goes=place(image_order),
    )
    parts = swapped(weighted, ("cond", "kern"), image_order)
    low, high = call(bounds_kernel, (shape((32, 128), F32),) * 2, parts, came=place(image_order))
    return (low[None], high[None])


def solution(mesh):
    placed = (P(None, "tile", None), P(None, "cond", "kern", "tile", None), P("cond", "kern"))
    return jax.shard_map(
        local,
        mesh=mesh,
        in_specs=placed,
        out_specs=(P(None, "tile", "kern"), P(None, "tile", "kern")),
        check_vma=False,
    )
```

```python
import functools
import math

import jax
import jax.numpy as jnp
import numpy as np
from jax import lax
from jax.experimental import pallas as pl
from jax.experimental.pallas import tpu as pltpu
from jax.sharding import PartitionSpec as P

BF = jnp.bfloat16
F32 = jnp.float32
TN = (((0,), (0,)), ((), ()))
NN = (((1,), (0,)), ((), ()))
NT = (((1,), (1,)), ((), ()))


def ring_order(rings, length, first, step):
    return [
        ring * length + (first + step * at) % length
        for at in range(length)
        for ring in reversed(range(rings))
    ]


def tables(length, count):
    pixel = np.arange(length, dtype=np.int64)[:, None]
    freq = np.arange(count, dtype=np.int64)[None, :] - count // 2
    phase = np.mod(pixel * freq, length).astype(np.float32) * np.float32(2.0 * math.pi / length)
    factor = np.float32(1.0 / math.sqrt(length))
    return (
        (np.cos(phase) * factor).astype(BF),
        (np.sin(phase) * factor).astype(BF),
    )


def turned(re, im, quarters):
    quarters %= 4
    if quarters == 0:
        return re, im
    place = lax.broadcasted_iota(jnp.int32, re.shape, 1) % 4
    odd = place % 2 == 1
    if quarters == 2:
        return jnp.where(odd, -re, re), jnp.where(odd, -im, im)
    real, imag = jnp.where(odd, im, re), jnp.where(odd, re, im)
    early, late = (place == 1) | (place == 2), place >= 2
    if quarters == 3:
        early, late = late, early
    return jnp.where(early, -real, real), jnp.where(late, -imag, imag)


def summed(pairs):
    total_re, total_im = pairs[0]
    for re, im in pairs[1:]:
        total_re, total_im = total_re + re, total_im + im
    return total_re, total_im


def sided(re, im):
    rows = []
    for m in range(4):
        there_re, there_im = turned(re, im, m)
        rows += [jnp.concatenate([there_re, -there_im], axis=1), jnp.concatenate([there_im, there_re], axis=1)]
    return jnp.concatenate(rows, axis=0)


def dot(a, b, dims):
    return lax.dot_general(a, b, dims, preferred_element_type=F32)


def regroup(blocks, lanes):
    group = (lax.broadcasted_iota(jnp.int32, blocks[0].shape, 1) // 32) % 4
    outs = []
    for b in range(4):
        moved = [
            blk if q == b else pltpu.roll(blk, (32 * (q - b)) % lanes, 1)
            for q, blk in enumerate(blocks)
        ]
        low = jnp.where(group == 0, moved[0], moved[1])
        high = jnp.where(group == 2, moved[2], moved[3])
        outs.append(jnp.where(group < 2, low, high))
    return outs


def rows_kernel(
    mask_ref, rows_ref, table_ref, kern_ref, out_ref, table_out, kern_out, mask_buf, table_buf, sems
):
    pairs = [(mask_ref, mask_buf), (rows_ref, table_buf), (table_ref, table_out), (kern_ref, kern_out)]
    copies = [pltpu.make_async_copy(src, dst, sems.at[n]) for n, (src, dst) in enumerate(pairs)]
    for copy in copies:
        copy.start()
    for copy in copies[:2]:
        copy.wait()
    rows, pixels = mask_buf.shape
    near = pixels // 4
    both = jnp.concatenate([mask_buf[:, m * near : (m + 1) * near] for m in range(4)], axis=0)
    part = dot(both, table_buf[...], NN)
    count = part.shape[1] // 2
    parts = [part[m * rows : (m + 1) * rows] for m in range(4)]
    out = jnp.concatenate(
        summed([turned(p[:, :count], p[:, count:], -m) for m, p in enumerate(parts)]), axis=1
    )
    width = out.shape[1] // 4
    stacked = jnp.concatenate([out[:, g * width : (g + 1) * width] for g in range(4)], axis=0)
    out_ref[...] = stacked.T.astype(BF)
    for copy in copies[2:]:
        copy.wait()


def half_kernel(cols_ref, kern_ref, table_ref, out_ref, *, came, goes):
    tiles = cols_ref.shape[0] // 8
    count = kern_ref.shape[3]
    cols = cols_ref[...].astype(F32).reshape(tiles, 8, 128)
    blocks = [
        jnp.concatenate([cols[came[4 * D + b]] for D in range(tiles // 4)], axis=1) for b in range(4)
    ]
    groups = regroup(blocks, 32 * tiles)
    lines = jnp.concatenate(groups, axis=0).astype(BF)
    near = lines.shape[1] // 4
    lines = jnp.concatenate([lines[:, m * near : (m + 1) * near] for m in range(4)], axis=0)
    part = dot(lines, table_ref[...], NT)
    parts = []
    for m in range(4):
        top, low = part[32 * m : 32 * m + 16], part[32 * m + 16 : 32 * m + 32]
        parts.append(
            turned(top[:, :count] + low[:, count:], low[:, :count] - top[:, count:], -m)
        )
    spec_re, spec_im = summed(parts)
    items = kern_ref.shape[1]
    fre, fim = [], []
    for n in range(items):
        kre = kern_ref[0, n].astype(F32)
        kim = kern_ref[1, n].astype(F32)
        fre.append((spec_re * kre - spec_im * kim).astype(BF))
        fim.append((spec_re * kim + spec_im * kre).astype(BF))
    lhs = sided(jnp.concatenate(fre, axis=0), jnp.concatenate(fim, axis=0))
    fields = dot(lhs, table_ref[...], NN)
    for side in range(4):
        start = side * 32 * items
        block = [fields[start + 16 * n : start + 16 * n + 16] for n in range(2 * items)]
        quads = (block[:4], block[items : items + 4], block[4:items] + block[items + 4 :])
        for at, quad in enumerate(quads):
            for b, moved in enumerate(regroup(quad, near)):
                moved = moved.astype(BF)
                for D in range(near // 128):
                    d = side * tiles // 4 + 4 * D + b
                    out_ref[goes[d], 16 * at : 16 * at + 16] = moved[:, 128 * D : 128 * D + 128]


def power_kernel(half_ref, weight_ref, table_ref, out_ref, *, came, goes):
    tiles = half_ref.shape[0]
    conds, kerns = weight_ref.shape
    half = [half_ref[came[t]] for t in range(tiles)]
    quad = [jnp.concatenate([h[16 * q : 16 * q + 16] for h in half], axis=0).T for q in range(3)]
    half_re = jnp.concatenate([quad[0], quad[2][:64]], axis=0)
    half_im = jnp.concatenate([quad[1], quad[2][64:]], axis=0)
    fields = dot(sided(half_re, half_im), table_ref[...], NN)
    count = half_re.shape[0]
    near = fields.shape[1] // 128
    for side in range(4):
        field_re = fields[2 * side * count : (2 * side + 1) * count]
        field_im = fields[(2 * side + 1) * count : (2 * side + 2) * count]
        power = field_re * field_re + field_im * field_im
        for c in range(conds):
            total = None
            for k in range(kerns):
                n = c * kerns + k
                term = power[32 * n : 32 * n + 32] * weight_ref[c, k]
                total = term if total is None else total + term
            total = total.astype(BF)
            for d in range(out_ref.shape[0]):
                if d % (4 * near) // near == side:
                    at = d % near * 128
                    out_ref[goes[d], 32 * c : 32 * c + 32] = total[:, at : at + 128]


def bounds_kernel(parts_ref, low_ref, high_ref, *, came):
    halves = []
    kern = parts_ref.shape[0] // 2
    for group in range(2):
        total = parts_ref[came[group * kern]].astype(F32)
        for s in range(1, kern):
            total = total + parts_ref[came[group * kern + s]].astype(F32)
        halves += [total[:32], total[32:]]
    low_ref[...] = jnp.minimum(jnp.minimum(halves[0], halves[1]), jnp.minimum(halves[2], halves[3]))
    high_ref[...] = jnp.maximum(jnp.maximum(halves[0], halves[1]), jnp.maximum(halves[2], halves[3]))


def call(body, shapes, *args, spaces={}, scratch=(), **places):
    return pl.pallas_call(
        functools.partial(body, **places),
        out_shape=shapes,
        in_specs=[
            pl.BlockSpec(memory_space=spaces.get(n, pltpu.VMEM)) for n in range(len(args))
        ],
        out_specs=jax.tree.map(lambda _: pl.BlockSpec(memory_space=pltpu.VMEM), shapes),
        scratch_shapes=scratch,
        compiler_params=pltpu.CompilerParams(vmem_limit_bytes=48 * 1024 * 1024),
        name=body.__name__,
    )(*args)


def swapped(blocks, axis, order):
    return lax.all_to_all(
        blocks, axis, split_axis=0, concat_axis=0, tiled=True, axis_index_groups=[order]
    )


def place(order):
    return [order.index(member) for member in range(len(order))]


def local(mask, kernels, kernel_weights):
    _, rows, pixels = mask.shape
    conds, kerns = kernel_weights.shape
    count = kernels.shape[4]
    tiles, groups = lax.axis_size("tile"), lax.axis_size("kern") * lax.axis_size("cond")
    cos_table, sin_table = tables(pixels, count)
    table = jnp.asarray(np.concatenate([cos_table, sin_table], axis=1)[: pixels // 4].T)
    tile_order = ring_order(2, tiles // 2, 10, 7)
    image_order = ring_order(1, groups, 13, 1)
    order = np.arange(count).reshape(tiles, 2, 8)[tile_order].transpose(1, 0, 2).reshape(-1)
    row_table = np.concatenate([cos_table[:, order], -sin_table[:, order]], axis=1)
    row_table = jnp.asarray(row_table[: pixels // 4])
    shape = jax.ShapeDtypeStruct

    kern = kernels.reshape(2, conds * kerns, kernels.shape[3], count)
    sent, table, kern = call(
        rows_kernel,
        (shape((8 * tiles, 128), BF), shape(table.shape, BF), shape(kern.shape, BF)),
        *(pltpu.with_memory_space_constraint(a, pltpu.HBM) for a in (mask[0], row_table, table, kern)),
        spaces={n: pltpu.HBM for n in range(4)},
        scratch=[
            pltpu.VMEM((rows, pixels), BF),
            pltpu.VMEM(row_table.shape, BF),
            pltpu.SemaphoreType.DMA((4,)),
        ],
    )
    cols = swapped(sent, "tile", tile_order)
    half = call(
        half_kernel,
        shape((tiles, 48, 128), BF),
        cols,
        kern,
        table,
        came=place(tile_order),
        goes=place(tile_order),
    )
    half = swapped(half, "tile", tile_order)
    weighted = call(
        power_kernel,
        shape((groups, 64, 128), BF),
        half,
        kernel_weights,
        table,
        spaces={1: pltpu.SMEM},
        came=place(tile_order),
        goes=place(image_order),
    )
    parts = swapped(weighted, ("cond", "kern"), image_order)
    low, high = call(bounds_kernel, (shape((32, 128), F32),) * 2, parts, came=place(image_order))
    return (low[None], high[None])


def solution(mesh):
    placed = (P(None, "tile", None), P(None, "cond", "kern", "tile", None), P("cond", "kern"))
    return jax.shard_map(
        local,
        mesh=mesh,
        in_specs=placed,
        out_specs=(P(None, "tile", "kern"), P(None, "tile", "kern")),
        check_vma=False,
    )
```

```python
import functools
import math

import jax
import jax.numpy as jnp
import numpy as np
from jax import lax
from jax.experimental import pallas as pl
from jax.experimental.pallas import tpu as pltpu
from jax.sharding import PartitionSpec as P

BF = jnp.bfloat16
F32 = jnp.float32
TN = (((0,), (0,)), ((), ()))
NN = (((1,), (0,)), ((), ()))
NT = (((1,), (1,)), ((), ()))


def ring_order(rings, length, first, step):
    return [
        ring * length + (first + step * at) % length
        for at in range(length)
        for ring in reversed(range(rings))
    ]


def tables(length, count):
    pixel = np.arange(length, dtype=np.int64)[:, None]
    freq = np.arange(count, dtype=np.int64)[None, :] - count // 2
    phase = np.mod(pixel * freq, length).astype(np.float32) * np.float32(2.0 * math.pi / length)
    factor = np.float32(1.0 / math.sqrt(length))
    return (
        (np.cos(phase) * factor).astype(BF),
        (np.sin(phase) * factor).astype(BF),
    )


def turned(re, im, quarters):
    quarters %= 4
    if quarters == 0:
        return re, im
    place = lax.broadcasted_iota(jnp.int32, re.shape, 1) % 4
    odd = place % 2 == 1
    if quarters == 2:
        return jnp.where(odd, -re, re), jnp.where(odd, -im, im)
    real, imag = jnp.where(odd, im, re), jnp.where(odd, re, im)
    early, late = (place == 1) | (place == 2), place >= 2
    if quarters == 3:
        early, late = late, early
    return jnp.where(early, -real, real), jnp.where(late, -imag, imag)


def summed(pairs):
    total_re, total_im = pairs[0]
    for re, im in pairs[1:]:
        total_re, total_im = total_re + re, total_im + im
    return total_re, total_im


def sided(re, im):
    rows = []
    for m in range(4):
        there_re, there_im = turned(re, im, m)
        rows += [jnp.concatenate([there_re, -there_im], axis=1), jnp.concatenate([there_im, there_re], axis=1)]
    return jnp.concatenate(rows, axis=0)


def dot(a, b, dims):
    return lax.dot_general(a, b, dims, preferred_element_type=F32)


def regroup(blocks, lanes):
    group = (lax.broadcasted_iota(jnp.int32, blocks[0].shape, 1) // 32) % 4
    outs = []
    for b in range(4):
        moved = [
            blk if q == b else pltpu.roll(blk, (32 * (q - b)) % lanes, 1)
            for q, blk in enumerate(blocks)
        ]
        low = jnp.where(group == 0, moved[0], moved[1])
        high = jnp.where(group == 2, moved[2], moved[3])
        outs.append(jnp.where(group < 2, low, high))
    return outs


def rows_kernel(
    mask_ref, rows_ref, table_ref, kern_ref, out_ref, table_out, kern_out, mask_buf, table_buf, sems
):
    pairs = [(mask_ref, mask_buf), (rows_ref, table_buf), (table_ref, table_out), (kern_ref, kern_out)]
    copies = [pltpu.make_async_copy(src, dst, sems.at[n]) for n, (src, dst) in enumerate(pairs)]
    for copy in copies[:2]:
        copy.start()
    for copy in copies[2:]:
        copy.start(priority=1)
    for copy in copies[:2]:
        copy.wait()
    rows, pixels = mask_buf.shape
    near = pixels // 4
    both = jnp.concatenate([mask_buf[:, m * near : (m + 1) * near] for m in range(4)], axis=0)
    part = dot(both, table_buf[...], NN)
    count = part.shape[1] // 2
    parts = [part[m * rows : (m + 1) * rows] for m in range(4)]
    out = jnp.concatenate(
        summed([turned(p[:, :count], p[:, count:], -m) for m, p in enumerate(parts)]), axis=1
    )
    width = out.shape[1] // 4
    stacked = jnp.concatenate([out[:, g * width : (g + 1) * width] for g in range(4)], axis=0)
    out_ref[...] = stacked.T.astype(BF)
    for copy in copies[2:]:
        copy.wait()


def half_kernel(cols_ref, kern_ref, table_ref, out_ref, *, came, goes):
    tiles = cols_ref.shape[0] // 8
    count = kern_ref.shape[3]
    cols = cols_ref[...].astype(F32).reshape(tiles, 8, 128)
    blocks = [
        jnp.concatenate([cols[came[4 * D + b]] for D in range(tiles // 4)], axis=1) for b in range(4)
    ]
    groups = regroup(blocks, 32 * tiles)
    lines = jnp.concatenate(groups, axis=0).astype(BF)
    near = lines.shape[1] // 4
    lines = jnp.concatenate([lines[:, m * near : (m + 1) * near] for m in range(4)], axis=0)
    part = dot(lines, table_ref[...], NT)
    parts = []
    for m in range(4):
        top, low = part[32 * m : 32 * m + 16], part[32 * m + 16 : 32 * m + 32]
        parts.append(
            turned(top[:, :count] + low[:, count:], low[:, :count] - top[:, count:], -m)
        )
    spec_re, spec_im = summed(parts)
    items = kern_ref.shape[1]
    fre, fim = [], []
    for n in range(items):
        kre = kern_ref[0, n].astype(F32)
        kim = kern_ref[1, n].astype(F32)
        fre.append((spec_re * kre - spec_im * kim).astype(BF))
        fim.append((spec_re * kim + spec_im * kre).astype(BF))
    lhs = sided(jnp.concatenate(fre, axis=0), jnp.concatenate(fim, axis=0))
    fields = dot(lhs, table_ref[...], NN)
    for side in range(4):
        start = side * 32 * items
        block = [fields[start + 16 * n : start + 16 * n + 16] for n in range(2 * items)]
        quads = (block[:4], block[items : items + 4], block[4:items] + block[items + 4 :])
        for at, quad in enumerate(quads):
            for b, moved in enumerate(regroup(quad, near)):
                moved = moved.astype(BF)
                for D in range(near // 128):
                    d = side * tiles // 4 + 4 * D + b
                    out_ref[goes[d], 16 * at : 16 * at + 16] = moved[:, 128 * D : 128 * D + 128]


def power_kernel(half_ref, weight_ref, table_ref, out_ref, *, came, goes):
    tiles = half_ref.shape[0]
    conds, kerns = weight_ref.shape
    half = [half_ref[came[t]] for t in range(tiles)]
    quad = [jnp.concatenate([h[16 * q : 16 * q + 16] for h in half], axis=0).T for q in range(3)]
    half_re = jnp.concatenate([quad[0], quad[2][:64]], axis=0)
    half_im = jnp.concatenate([quad[1], quad[2][64:]], axis=0)
    fields = dot(sided(half_re, half_im), table_ref[...], NN)
    count = half_re.shape[0]
    near = fields.shape[1] // 128
    for side in range(4):
        field_re = fields[2 * side * count : (2 * side + 1) * count]
        field_im = fields[(2 * side + 1) * count : (2 * side + 2) * count]
        power = field_re * field_re + field_im * field_im
        for c in range(conds):
            total = None
            for k in range(kerns):
                n = c * kerns + k
                term = power[32 * n : 32 * n + 32] * weight_ref[c, k]
                total = term if total is None else total + term
            total = total.astype(BF)
            for d in range(out_ref.shape[0]):
                if d % (4 * near) // near == side:
                    at = d % near * 128
                    out_ref[goes[d], 32 * c : 32 * c + 32] = total[:, at : at + 128]


def bounds_kernel(parts_ref, low_ref, high_ref, *, came):
    halves = []
    kern = parts_ref.shape[0] // 2
    for group in range(2):
        total = parts_ref[came[group * kern]].astype(F32)
        for s in range(1, kern):
            total = total + parts_ref[came[group * kern + s]].astype(F32)
        halves += [total[:32], total[32:]]
    low_ref[...] = jnp.minimum(jnp.minimum(halves[0], halves[1]), jnp.minimum(halves[2], halves[3]))
    high_ref[...] = jnp.maximum(jnp.maximum(halves[0], halves[1]), jnp.maximum(halves[2], halves[3]))


def call(body, shapes, *args, spaces={}, scratch=(), **places):
    return pl.pallas_call(
        functools.partial(body, **places),
        out_shape=shapes,
        in_specs=[
            pl.BlockSpec(memory_space=spaces.get(n, pltpu.VMEM)) for n in range(len(args))
        ],
        out_specs=jax.tree.map(lambda _: pl.BlockSpec(memory_space=pltpu.VMEM), shapes),
        scratch_shapes=scratch,
        compiler_params=pltpu.CompilerParams(vmem_limit_bytes=48 * 1024 * 1024),
        name=body.__name__,
    )(*args)


def swapped(blocks, axis, order):
    return lax.all_to_all(
        blocks, axis, split_axis=0, concat_axis=0, tiled=True, axis_index_groups=[order]
    )


def place(order):
    return [order.index(member) for member in range(len(order))]


def local(mask, kernels, kernel_weights):
    _, rows, pixels = mask.shape
    conds, kerns = kernel_weights.shape
    count = kernels.shape[4]
    tiles, groups = lax.axis_size("tile"), lax.axis_size("kern") * lax.axis_size("cond")
    cos_table, sin_table = tables(pixels, count)
    table = jnp.asarray(np.concatenate([cos_table, sin_table], axis=1)[: pixels // 4].T)
    tile_order = ring_order(2, tiles // 2, 10, 7)
    rows_order = ring_order(2, tiles // 2, 11, 7)
    image_order = ring_order(1, groups, 13, 1)
    order = np.arange(count).reshape(tiles, 2, 8)[rows_order].transpose(1, 0, 2).reshape(-1)
    row_table = np.concatenate([cos_table[:, order], -sin_table[:, order]], axis=1)
    row_table = jnp.asarray(row_table[: pixels // 4])
    shape = jax.ShapeDtypeStruct

    kern = kernels.reshape(2, conds * kerns, kernels.shape[3], count)
    sent, table, kern = call(
        rows_kernel,
        (shape((8 * tiles, 128), BF), shape(table.shape, BF), shape(kern.shape, BF)),
        *(pltpu.with_memory_space_constraint(a, pltpu.HBM) for a in (mask[0], row_table, table, kern)),
        spaces={n: pltpu.HBM for n in range(4)},
        scratch=[
            pltpu.VMEM((rows, pixels), BF),
            pltpu.VMEM(row_table.shape, BF),
            pltpu.SemaphoreType.DMA((4,)),
        ],
    )
    cols = swapped(sent, "tile", rows_order)
    half = call(
        half_kernel,
        shape((tiles, 48, 128), BF),
        cols,
        kern,
        table,
        came=place(rows_order),
        goes=place(tile_order),
    )
    half = swapped(half, "tile", tile_order)
    weighted = call(
        power_kernel,
        shape((groups, 64, 128), BF),
        half,
        kernel_weights,
        table,
        spaces={1: pltpu.SMEM},
        came=place(tile_order),
        goes=place(image_order),
    )
    parts = swapped(weighted, ("cond", "kern"), image_order)
    low, high = call(bounds_kernel, (shape((32, 128), F32),) * 2, parts, came=place(image_order))
    return (low[None], high[None])


def solution(mesh):
    placed = (P(None, "tile", None), P(None, "cond", "kern", "tile", None), P("cond", "kern"))
    return jax.shard_map(
        local,
        mesh=mesh,
        in_specs=placed,
        out_specs=(P(None, "tile", "kern"), P(None, "tile", "kern")),
        check_vma=False,
    )
```

```python
import functools
import math

import jax
import jax.numpy as jnp
import numpy as np
from jax import lax
from jax.experimental import pallas as pl
from jax.experimental.pallas import tpu as pltpu
from jax.sharding import PartitionSpec as P

BF = jnp.bfloat16
F32 = jnp.float32
TN = (((0,), (0,)), ((), ()))
NN = (((1,), (0,)), ((), ()))
NT = (((1,), (1,)), ((), ()))


def ring_order(rings, length, first, step):
    return [
        ring * length + (first + step * at) % length
        for at in range(length)
        for ring in reversed(range(rings))
    ]


def tables(length, count):
    pixel = np.arange(length, dtype=np.int64)[:, None]
    freq = np.arange(count, dtype=np.int64)[None, :] - count // 2
    phase = np.mod(pixel * freq, length).astype(np.float32) * np.float32(2.0 * math.pi / length)
    factor = np.float32(1.0 / math.sqrt(length))
    return (
        (np.cos(phase) * factor).astype(BF),
        (np.sin(phase) * factor).astype(BF),
    )


def turned(re, im, quarters):
    quarters %= 4
    if quarters == 0:
        return re, im
    place = lax.broadcasted_iota(jnp.int32, re.shape, 1) % 4
    odd = place % 2 == 1
    if quarters == 2:
        return jnp.where(odd, -re, re), jnp.where(odd, -im, im)
    real, imag = jnp.where(odd, im, re), jnp.where(odd, re, im)
    early, late = (place == 1) | (place == 2), place >= 2
    if quarters == 3:
        early, late = late, early
    return jnp.where(early, -real, real), jnp.where(late, -imag, imag)


def summed(pairs):
    total_re, total_im = pairs[0]
    for re, im in pairs[1:]:
        total_re, total_im = total_re + re, total_im + im
    return total_re, total_im


def sided(re, im):
    rows = []
    for m in range(4):
        there_re, there_im = turned(re, im, m)
        rows += [jnp.concatenate([there_re, -there_im], axis=1), jnp.concatenate([there_im, there_re], axis=1)]
    return jnp.concatenate(rows, axis=0)


def dot(a, b, dims):
    return lax.dot_general(a, b, dims, preferred_element_type=F32)


def regroup(blocks, lanes):
    group = (lax.broadcasted_iota(jnp.int32, blocks[0].shape, 1) // 32) % 4
    outs = []
    for b in range(4):
        moved = [
            blk if q == b else pltpu.roll(blk, (32 * (q - b)) % lanes, 1)
            for q, blk in enumerate(blocks)
        ]
        low = jnp.where(group == 0, moved[0], moved[1])
        high = jnp.where(group == 2, moved[2], moved[3])
        outs.append(jnp.where(group < 2, low, high))
    return outs


def rows_kernel(
    mask_ref, rows_ref, table_ref, kern_ref, out_ref, table_out, kern_out, mask_buf, table_buf, sems
):
    pairs = [(mask_ref, mask_buf), (rows_ref, table_buf), (table_ref, table_out), (kern_ref, kern_out)]
    pieces = [(mask_ref, mask_buf)]
    for src, dst in pairs[1:]:
        step = src.shape[0] // 2
        for at in (0, step):
            pieces.append((src.at[pl.ds(at, step)], dst.at[pl.ds(at, step)]))
    copies = [pltpu.make_async_copy(src, dst, sems.at[n]) for n, (src, dst) in enumerate(pieces)]
    for copy in copies[:3]:
        copy.start()
    for copy in copies[3:]:
        copy.start(priority=1)
    for copy in copies[:3]:
        copy.wait()
    rows, pixels = mask_buf.shape
    near = pixels // 4
    both = jnp.concatenate([mask_buf[:, m * near : (m + 1) * near] for m in range(4)], axis=0)
    part = dot(both, table_buf[...], NN)
    count = part.shape[1] // 2
    parts = [part[m * rows : (m + 1) * rows] for m in range(4)]
    out = jnp.concatenate(
        summed([turned(p[:, :count], p[:, count:], -m) for m, p in enumerate(parts)]), axis=1
    )
    width = out.shape[1] // 4
    stacked = jnp.concatenate([out[:, g * width : (g + 1) * width] for g in range(4)], axis=0)
    out_ref[...] = stacked.T.astype(BF)
    for copy in copies[3:]:
        copy.wait()


def half_kernel(cols_ref, kern_ref, table_ref, out_ref, *, came, goes):
    tiles = cols_ref.shape[0] // 8
    count = kern_ref.shape[3]
    cols = cols_ref[...].astype(F32).reshape(tiles, 8, 128)
    blocks = [
        jnp.concatenate([cols[came[4 * D + b]] for D in range(tiles // 4)], axis=1) for b in range(4)
    ]
    groups = regroup(blocks, 32 * tiles)
    lines = jnp.concatenate(groups, axis=0).astype(BF)
    near = lines.shape[1] // 4
    lines = jnp.concatenate([lines[:, m * near : (m + 1) * near] for m in range(4)], axis=0)
    part = dot(lines, table_ref[...], NT)
    parts = []
    for m in range(4):
        top, low = part[32 * m : 32 * m + 16], part[32 * m + 16 : 32 * m + 32]
        parts.append(
            turned(top[:, :count] + low[:, count:], low[:, :count] - top[:, count:], -m)
        )
    spec_re, spec_im = summed(parts)
    items = kern_ref.shape[1]
    fre, fim = [], []
    for n in range(items):
        kre = kern_ref[0, n].astype(F32)
        kim = kern_ref[1, n].astype(F32)
        fre.append((spec_re * kre - spec_im * kim).astype(BF))
        fim.append((spec_re * kim + spec_im * kre).astype(BF))
    lhs = sided(jnp.concatenate(fre, axis=0), jnp.concatenate(fim, axis=0))
    fields = dot(lhs, table_ref[...], NN)
    for side in range(4):
        start = side * 32 * items
        block = [fields[start + 16 * n : start + 16 * n + 16] for n in range(2 * items)]
        quads = (block[:4], block[items : items + 4], block[4:items] + block[items + 4 :])
        for at, quad in enumerate(quads):
            for b, moved in enumerate(regroup(quad, near)):
                moved = moved.astype(BF)
                for D in range(near // 128):
                    d = side * tiles // 4 + 4 * D + b
                    out_ref[goes[d], 16 * at : 16 * at + 16] = moved[:, 128 * D : 128 * D + 128]


def power_kernel(half_ref, weight_ref, table_ref, out_ref, *, came, goes):
    tiles = half_ref.shape[0]
    conds, kerns = weight_ref.shape
    half = [half_ref[came[t]] for t in range(tiles)]
    quad = [jnp.concatenate([h[16 * q : 16 * q + 16] for h in half], axis=0).T for q in range(3)]
    half_re = jnp.concatenate([quad[0], quad[2][:64]], axis=0)
    half_im = jnp.concatenate([quad[1], quad[2][64:]], axis=0)
    fields = dot(sided(half_re, half_im), table_ref[...], NN)
    count = half_re.shape[0]
    near = fields.shape[1] // 128
    for side in range(4):
        field_re = fields[2 * side * count : (2 * side + 1) * count]
        field_im = fields[(2 * side + 1) * count : (2 * side + 2) * count]
        power = field_re * field_re + field_im * field_im
        for c in range(conds):
            total = None
            for k in range(kerns):
                n = c * kerns + k
                term = power[32 * n : 32 * n + 32] * weight_ref[c, k]
                total = term if total is None else total + term
            total = total.astype(BF)
            for d in range(out_ref.shape[0]):
                if d % (4 * near) // near == side:
                    at = d % near * 128
                    out_ref[goes[d], 32 * c : 32 * c + 32] = total[:, at : at + 128]


def bounds_kernel(parts_ref, low_ref, high_ref, *, came):
    halves = []
    kern = parts_ref.shape[0] // 2
    for group in range(2):
        total = parts_ref[came[group * kern]].astype(F32)
        for s in range(1, kern):
            total = total + parts_ref[came[group * kern + s]].astype(F32)
        halves += [total[:32], total[32:]]
    low_ref[...] = jnp.minimum(jnp.minimum(halves[0], halves[1]), jnp.minimum(halves[2], halves[3]))
    high_ref[...] = jnp.maximum(jnp.maximum(halves[0], halves[1]), jnp.maximum(halves[2], halves[3]))


def call(body, shapes, *args, spaces={}, scratch=(), **places):
    return pl.pallas_call(
        functools.partial(body, **places),
        out_shape=shapes,
        in_specs=[
            pl.BlockSpec(memory_space=spaces.get(n, pltpu.VMEM)) for n in range(len(args))
        ],
        out_specs=jax.tree.map(lambda _: pl.BlockSpec(memory_space=pltpu.VMEM), shapes),
        scratch_shapes=scratch,
        compiler_params=pltpu.CompilerParams(vmem_limit_bytes=48 * 1024 * 1024),
        name=body.__name__,
    )(*args)


def swapped(blocks, axis, order):
    return lax.all_to_all(
        blocks, axis, split_axis=0, concat_axis=0, tiled=True, axis_index_groups=[order]
    )


def place(order):
    return [order.index(member) for member in range(len(order))]


def local(mask, kernels, kernel_weights):
    _, rows, pixels = mask.shape
    conds, kerns = kernel_weights.shape
    count = kernels.shape[4]
    tiles, groups = lax.axis_size("tile"), lax.axis_size("kern") * lax.axis_size("cond")
    cos_table, sin_table = tables(pixels, count)
    table = jnp.asarray(np.concatenate([cos_table, sin_table], axis=1)[: pixels // 4].T)
    tile_order = ring_order(2, tiles // 2, 10, 7)
    rows_order = ring_order(2, tiles // 2, 11, 7)
    image_order = ring_order(1, groups, 13, 1)
    order = np.arange(count).reshape(tiles, 2, 8)[rows_order].transpose(1, 0, 2).reshape(-1)
    row_table = np.concatenate([cos_table[:, order], -sin_table[:, order]], axis=1)
    row_table = jnp.asarray(row_table[: pixels // 4])
    shape = jax.ShapeDtypeStruct

    kern = kernels.reshape(2, conds * kerns, kernels.shape[3], count)
    sent, table, kern = call(
        rows_kernel,
        (shape((8 * tiles, 128), BF), shape(table.shape, BF), shape(kern.shape, BF)),
        *(pltpu.with_memory_space_constraint(a, pltpu.HBM) for a in (mask[0], row_table, table, kern)),
        spaces={n: pltpu.HBM for n in range(4)},
        scratch=[
            pltpu.VMEM((rows, pixels), BF),
            pltpu.VMEM(row_table.shape, BF),
            pltpu.SemaphoreType.DMA((7,)),
        ],
    )
    cols = swapped(sent, "tile", rows_order)
    half = call(
        half_kernel,
        shape((tiles, 48, 128), BF),
        cols,
        kern,
        table,
        came=place(rows_order),
        goes=place(tile_order),
    )
    half = swapped(half, "tile", tile_order)
    weighted = call(
        power_kernel,
        shape((groups, 64, 128), BF),
        half,
        kernel_weights,
        table,
        spaces={1: pltpu.SMEM},
        came=place(tile_order),
        goes=place(image_order),
    )
    parts = swapped(weighted, ("cond", "kern"), image_order)
    low, high = call(bounds_kernel, (shape((32, 128), F32),) * 2, parts, came=place(image_order))
    return (low[None], high[None])


def solution(mesh):
    placed = (P(None, "tile", None), P(None, "cond", "kern", "tile", None), P("cond", "kern"))
    return jax.shard_map(
        local,
        mesh=mesh,
        in_specs=placed,
        out_specs=(P(None, "tile", "kern"), P(None, "tile", "kern")),
        check_vma=False,
    )
```
